768 devices in a mesh: group: 2 (over core), face: 6 (over z_lo), tile: 64 (over y, x, z_hi).
Axes of the slice: x: 4, y: 8, z: 12 (z_hi: 2, z_lo: 6; z = z_hi * 6 + z_lo), core: 2. Of those that a mesh axis runs over, the one named last changes fastest.
Arguments:
- tracers: float32 [6, 128, 8, 16, 316], P('face', ('group', 'tile')), may hold values from -6 to 6
- wind_field: float32 [6, 128, 8, 16, 158], P('face', ('group', 'tile')), may hold values from -0.45 to 0.45
- face_links: int32 [6, 4, 3], replicated, may hold values from 0 to 5, as said below
- owner_map: int32 [6, 128, 128, 1], P('face', ('group', 'tile')), may hold values from 0 to 63; in each aligned block of 128 rows (0 to 127, 128 to 255, ..., all dimensions but the last counted through in order) at most 4 rows name the same one
- first_layer: bfloat16 [64, 632, 512], P('tile'), may hold values from -0.25 to 0.25
- middle_layer: bfloat16 [64, 512, 512], P('tile'), may hold values from -0.25 to 0.25
- last_layer: bfloat16 [64, 512, 316], P('tile'), may hold values from -0.25 to 0.25
Outputs:
- updated: float32 [6, 128, 8, 16, 316], P('face', ('group', 'tile'))
The draws below stay inside these ranges and needn't reach their ends.
Inputs may be any that keep to these rules, and one draw needn't show every extreme that they name: `face_links`: the table describes the edges of a cube: [f, e] gives the face across edge e of face f (e: 0 west, 1 east, 2 south, 3 north), the edge of that face on the shared boundary, and 1 if positions along the boundary run in opposite directions on the two faces, else 0. For some f, faces f and (f + 3) % 6 share an edge where the west edge of one meets the east edge of the other with positions running the same way. `owner_map`: among the 128 columns of one block of one face, no owner is named by more than 4 columns.
All inputs are finite; a program needn't handle non-finite values.
Results may differ from the reference program's by a relative error of at most 0.0016.
Values may be sent and summed in bfloat16 or wider, within the bound.
A program may use at most 32 MiB of HBM per device.

```python
import math
import jax
import jax.numpy as jnp
import numpy as np
from jax import lax

LEV = 79
HID = 512
FACES = 6
ACROSS = 8
COLS_BLK = 16
NSIDE = 128
NB = 128
ROWS_BLK = 8
EXPERTS = 64
CAP = 4


def draw_face_links(key, part):
    normals = jnp.array([[1, 0, 0], [0, 1, 0], [-1, 0, 0], [0, -1, 0], [0, 0, 1], [0, 0, -1]], jnp.int32)
    tangent_x = jnp.array([[0, 1, 0], [-1, 0, 0], [0, -1, 0], [1, 0, 0], [1, 0, 0], [0, 1, 0]], jnp.int32)
    tangent_y = jnp.array([[0, 0, 1], [0, 0, 1], [0, 0, 1], [0, 0, 1], [0, 1, 0], [1, 0, 0]], jnp.int32)
    turn_key, label_key, order_key = jax.random.split(jax.random.fold_in(key, 11), 3)
    rotations = jax.random.randint(turn_key, (6,), 0, 4)
    face_ids = jnp.arange(6, dtype=jnp.int32)
    rotations = jnp.where((face_ids == 0) | (face_ids == 3), 0, rotations)
    for repeat in range(3):
        rotate = (rotations > repeat)[:, None]
        tangent_x, tangent_y = (jnp.where(rotate, tangent_y, tangent_x), jnp.where(rotate, -tangent_x, tangent_y))
    outward = jnp.stack([-tangent_x, tangent_x, -tangent_y, tangent_y], axis=1)
    along_edge = jnp.stack([tangent_y, tangent_y, tangent_x, tangent_x], axis=1)
    matches = jnp.all(outward[:, :, None, :] == normals[None, None, :, :], axis=-1)
    across = jnp.sum(jnp.where(matches, jnp.arange(6, dtype=jnp.int32)[None, None, :], 0), axis=-1).astype(jnp.int32)
    facing = jnp.all(outward[across] == normals[:, None, None, :], axis=-1)
    neighbour_edge = jnp.sum(jnp.where(facing, jnp.arange(4, dtype=jnp.int32)[None, None, :], 0), axis=-1).astype(jnp.int32)
    opposed = jnp.sum(along_edge * along_edge[across, neighbour_edge], axis=-1)
    opposed = jnp.where(opposed < 0, 1, 0).astype(jnp.int32)
    first_label = jax.random.randint(label_key, (), 0, 6).astype(jnp.int32)
    others = (first_label + jnp.array([1, 2, 4, 5], jnp.int32)) % 6
    others = jax.random.permutation(order_key, others).astype(jnp.int32)
    labels = jnp.stack([first_label, others[0], others[1], (first_label + 3) % 6, others[2], others[3]]).astype(jnp.int32)
    entries = jnp.stack([labels[across], neighbour_edge, opposed], axis=-1).astype(jnp.int32)
    link_table = jnp.zeros((6, 4, 3), jnp.int32).at[labels].set(entries)
    return link_table


def levels(stream_key, extent, cuts, least, top_value):
    def one(position, shards_of):
        steps = jax.random.uniform(jax.random.fold_in(jax.random.fold_in(stream_key, 6), position), (shards_of,), jnp.float32, least / len(cuts), top_value / len(cuts))
        return jnp.repeat(jnp.exp(steps), extent[position] // shards_of).reshape((-1,) + (1,) * (len(extent) - position - 1))

    level = one(*cuts[0])
    for cut in cuts[1:]:
        level = level * one(*cut)
    return level


def shared_out(rng, own, number, rows, count, top, limit, skew):
    order = jax.random.permutation(rng, count)
    crowded, ordinary = shares(count, rows * top, limit, skew, True), shares(count, rows * top, limit, skew, False)
    places = jnp.arange(count)

    def named(sizes, rotation):
        used = int((sizes > 0).sum())
        fixed = max(1, used // 4)
        passed = fixed + (places - fixed + rotation * (used - fixed)) % max(1, count - fixed)
        return jnp.zeros((count,), jnp.int32).at[order[jnp.where(places < fixed, places, passed)]].set(jnp.asarray(sizes, jnp.int32))

    sizes = jnp.where(number % 4 == 0, named(crowded, number // 4), named(ordinary, number - number // 4 - 1))
    mixed = jax.random.permutation(jax.random.fold_in(own, 3), count)
    source_of, receiver = mixed[0:count // 2 * 2:2], mixed[1:count // 2 * 2:2]
    room = jnp.minimum(sizes[source_of] - 1, limit - sizes[receiver]) // 2
    room = jnp.where((source_of == order[0]) | (receiver == order[0]) | (sizes[receiver] == 0), 0, jnp.maximum(room, 0))
    passed = jax.random.randint(jax.random.fold_in(own, 4), (count // 2,), 0, 1 << 20) % (room + 1)
    sizes = sizes.at[source_of].add(-passed).at[receiver].add(passed)
    items = jnp.searchsorted(jnp.cumsum(sizes), jnp.arange(rows * top), side="right").astype(jnp.int32)
    table = items.reshape(top, rows).T
    table = table[jax.random.permutation(jax.random.fold_in(own, 1), rows)]
    rotation = jax.random.randint(jax.random.fold_in(own, 2), (rows, 1), 0, top)
    return jnp.take_along_axis(table, (jnp.arange(top)[None, :] + rotation) % top, axis=1)


def shares(count, total, bound, skew, full):
    loads = [(1 << 20) // math.isqrt(grade ** skew) + 1 for grade in range(1, count + 1)]
    largest = bound if full else min(bound, max(-(-total // count), total * loads[0] // sum(loads)))
    least = 1 if total - largest >= count - 1 else 0
    given, surplus = [largest] + [least] * (count - 1), total - largest - least * (count - 1)
    while surplus > 0:
        movable = [i for i in range(1, count) if given[i] < largest] or [i for i in range(1, count) if given[i] < bound]
        whole, remaining = sum([loads[i] for i in movable]), surplus
        for i in movable:
            addition = min(bound - given[i], max(1, remaining * loads[i] // whole), surplus)
            given[i] = given[i] + addition
            surplus = surplus - addition
    return np.array(given)


def scatter_about(stream_key, shape, width, limit, cuts=(), kind=jnp.bfloat16):
    values = width * jax.random.normal(stream_key, shape, jnp.float32)
    if cuts:
        values = values * levels(stream_key, shape, cuts, -0.22, 0.18)
    return jnp.clip(values, -limit, limit).astype(kind)


def setup_inputs(seed: int = 0) -> dict:
    key_list = jax.random.split(jax.random.key(seed), 8)
    tracers = scatter_about(key_list[0], (FACES, NB, ROWS_BLK, COLS_BLK, 4 * LEV), 1.0, 6.0, ((0, 6), (1, 128)), jnp.float32)
    wind_field = jnp.clip(jax.random.uniform(key_list[1], (FACES, NB, ROWS_BLK, COLS_BLK, 2 * LEV), jnp.float32, -0.45, 0.45) * levels(key_list[1], (FACES, NB, ROWS_BLK, COLS_BLK, 2 * LEV), ((0, 6), (1, 128)), -0.4, 0.0), -0.45, 0.45)
    face_links = draw_face_links(jax.random.fold_in(key_list[7], 71), 0)
    owner_map_keys = jax.random.split(jax.random.fold_in(key_list[3], 1), FACES * NB * (ROWS_BLK * COLS_BLK) // (ROWS_BLK * COLS_BLK))
    owner_map_turns = jax.random.permutation(jax.random.fold_in(key_list[3], 3), FACES * NB * (ROWS_BLK * COLS_BLK) // (ROWS_BLK * COLS_BLK))
    owner_map = jax.vmap(lambda own, number: shared_out(jax.random.fold_in(key_list[3], 2), own, number, ROWS_BLK * COLS_BLK, EXPERTS, 1, CAP, 2))(owner_map_keys, owner_map_turns).reshape((FACES, NB, ROWS_BLK * COLS_BLK, 1))
    first_layer = scatter_about(key_list[4], (EXPERTS, 8 * LEV, HID), (8 * LEV) ** -0.5, 0.25, ((0, 64),))
    middle_layer = scatter_about(key_list[5], (EXPERTS, HID, HID), HID ** -0.5, 0.25, ((0, 64),))
    last_layer = scatter_about(key_list[6], (EXPERTS, HID, 4 * LEV), HID ** -0.5, 0.25, ((0, 64),))
    return dict(tracers=tracers, wind_field=wind_field, face_links=face_links, owner_map=owner_map, first_layer=first_layer, middle_layer=middle_layer, last_layer=last_layer)


def block_order():
    positions = np.arange(NB)
    row_ids = positions // ACROSS
    col_ids = positions % ACROSS
    upper = (col_ids >= ACROSS // 2).astype(np.int64)
    within = np.where(upper == 1, ACROSS - 1 - col_ids, col_ids)
    order = upper * (NB // 2) + row_ids * (ACROSS // 2) + within
    inverse = np.zeros(NB, np.int64)
    inverse[order] = positions
    return order, inverse


def to_faces(blocked):
    order, inverse = block_order()
    count = blocked.shape[-1]
    placed = blocked[:, order]
    shaped = placed.reshape(FACES, NB // ACROSS, ACROSS, ROWS_BLK, COLS_BLK, count)
    return shaped.transpose(0, 1, 3, 2, 4, 5).reshape(FACES, NSIDE, NSIDE, count)


def face_to_blocks(field):
    order, inverse = block_order()
    count = field.shape[-1]
    shaped = field.reshape(NB // ACROSS, ROWS_BLK, ACROSS, COLS_BLK, count)
    positional = shaped.transpose(0, 2, 1, 3, 4).reshape(NB, ROWS_BLK, COLS_BLK, count)
    return positional[inverse]


def inflow(values, outward):
    shaped = values.reshape(values.shape[:-1] + (4, LEV))
    return (shaped * jnp.maximum(outward, 0.0)[..., None, :]).reshape(values.shape)


def split_flow(values, speed):
    shaped = values.reshape(values.shape[:-1] + (4, LEV))
    forward = (shaped * jnp.maximum(speed, 0.0)[..., None, :]).reshape(values.shape)
    backward = (shaped * jnp.minimum(speed, 0.0)[..., None, :]).reshape(values.shape)
    return forward, backward


def reference(tracers, wind_field, face_links, owner_map, first_layer, middle_layer, last_layer):
    fields = to_faces(tracers)
    winds = to_faces(wind_field)
    u_wind = winds[..., :LEV]
    v_wind = winds[..., LEV:]
    rims = jnp.stack([inflow(fields[:, :, 0], -u_wind[:, :, 0]), inflow(fields[:, :, -1], u_wind[:, :, -1]), inflow(fields[:, 0], -v_wind[:, 0]), inflow(fields[:, -1], v_wind[:, -1])], axis=1)
    first_wide = first_layer.astype(jnp.float32)
    middle_wide = middle_layer.astype(jnp.float32)
    last_wide = last_layer.astype(jnp.float32)

    def one_face(face_index):
        field = fields[face_index]
        u_here = u_wind[face_index]
        v_here = v_wind[face_index]
        ghosts = []
        for edge_id in range(4):
            link_row = face_links[face_index, edge_id]
            ghost = rims[link_row[0], link_row[1]]
            ghosts.append(jnp.where(link_row[2] == 1, ghost[::-1], ghost))
        east_flow, west_flow = split_flow(field, u_here)
        north_flow, south_flow = split_flow(field, v_here)
        flux_x = jnp.concatenate([ghosts[0][:, None], east_flow], axis=1) + jnp.concatenate([west_flow, -ghosts[1][:, None]], axis=1)
        flux_y = jnp.concatenate([ghosts[2][None], north_flow], axis=0) + jnp.concatenate([south_flow, -ghosts[3][None]], axis=0)
        advected = field - (flux_x[:, 1:] - flux_x[:, :-1]) - (flux_y[1:] - flux_y[:-1])
        inputs = jnp.concatenate([advected.astype(jnp.bfloat16), (advected - field).astype(jnp.bfloat16)], axis=-1)
        inputs = face_to_blocks(inputs).reshape(NB, ROWS_BLK * COLS_BLK, 8 * LEV)
        routes = owner_map[face_index, :, :, 0].astype(jnp.int32)
        picked = (routes[..., None] == jnp.arange(EXPERTS, dtype=jnp.int32)).astype(jnp.int32)
        ranking = jnp.sum(picked * (jnp.cumsum(picked, axis=1).astype(jnp.int32) - 1), axis=-1).astype(jnp.int32)
        slot_ids = routes * (NB * CAP) + jnp.arange(NB, dtype=jnp.int32)[:, None] * CAP + ranking
        slot_ids = slot_ids.reshape(-1).astype(jnp.int32)
        buffer = jnp.zeros((EXPERTS * NB * CAP, 8 * LEV), jnp.bfloat16).at[slot_ids].set(inputs.reshape(-1, 8 * LEV))
        buffer = buffer.reshape(EXPERTS, NB * CAP, 8 * LEV).astype(jnp.float32)
        hidden_one = jax.nn.silu(jnp.einsum("esf,efh->esh", buffer, first_wide)).astype(jnp.bfloat16)
        hidden_two = jax.nn.silu(jnp.einsum("esh,ehk->esk", hidden_one.astype(jnp.float32), middle_wide)).astype(jnp.bfloat16)
        tendency = jnp.einsum("esk,ekf->esf", hidden_two.astype(jnp.float32), last_wide).astype(jnp.bfloat16)
        tendency = tendency.reshape(-1, 4 * LEV)[slot_ids].reshape(NB, ROWS_BLK, COLS_BLK, 4 * LEV)
        return face_to_blocks(advected) + tendency.astype(jnp.float32)

    return lax.map(one_face, jnp.arange(FACES, dtype=jnp.int32))
```

```python
import functools

import jax
import jax.numpy as jnp
from jax import lax
from jax.experimental import pallas as pl
from jax.experimental.pallas import tpu as pltpu
from jax.sharding import PartitionSpec as P

MESH = pl.DeviceIdType.MESH
ROWS, COLS, LEV = 8, 16, 79
CELLS = ROWS * COLS
WIDE = 4 * LEV
PAD = 384
FEAT = 2 * WIDE
FPAD = 640
TILES = 64
CAP = 4
SLOTS = TILES * CAP
F32, BF16, I32 = jnp.float32, jnp.bfloat16, jnp.int32


def iota(shape, dim):
    return lax.broadcasted_iota(I32, shape, dim)


def onehot(condition):
    return jnp.where(condition, 1.0, 0.0).astype(BF16)


def silu(x):
    return x / (1.0 + jnp.exp(-x))


def dot(a, b):
    return jnp.dot(a, b, preferred_element_type=F32)


def place_of(col):
    lower = col < 4
    return jnp.where(lower, 0, 1), jnp.where(lower, col, 7 - col)


def kernel(
    q_ref, w_ref, links, owner_ref, first_hbm, middle_hbm, last_hbm,
    out_ref,
    first, middle, last,
    strip_v, strip_h, ghost_v, ghost_h,
    cand_v, cand_h, fwd_v, fwd_h, rim_v, rim_h,
    wide, outbox, inbox, reply, answers,
    wsem, halo_send, halo_recv, cand_send, cand_recv, rim_send_v, rim_send_h, rim_recv,
    a2a_send, a2a_recv, ret_send, ret_recv, own_sem,
):
    group, face, tile = (lax.axis_index(a) for a in ("group", "face", "tile"))
    row = tile // 4
    within = tile % 4
    col = jnp.where(group == 0, within, 7 - within)
    is_v = within == 0
    is_n = row == 15
    is_h = jnp.logical_or(row == 0, is_n)
    edge_v = group
    edge_h = jnp.where(is_n, 1, 0)

    loads = [
        pltpu.make_async_copy(first_hbm, first, wsem.at[0]),
        pltpu.make_async_copy(middle_hbm, middle, wsem.at[1]),
        pltpu.make_async_copy(last_hbm, last, wsem.at[2]),
    ]
    for load in loads:
        load.start()

    def device(r, c):
        g, k = place_of(c)
        return (g, face, r * 4 + k)

    halo = [
        (col > 0, device(row, col - 1), strip_v.at[0], ghost_v.at[1], halo_send.at[0], halo_recv.at[1]),
        (col < 7, device(row, col + 1), strip_v.at[1], ghost_v.at[0], halo_send.at[1], halo_recv.at[0]),
        (row > 0, device(row - 1, col), strip_h.at[0], ghost_h.at[1], halo_send.at[2], halo_recv.at[3]),
        (row < 15, device(row + 1, col), strip_h.at[1], ghost_h.at[0], halo_send.at[3], halo_recv.at[2]),
    ]
    relay = []

    def to_relay(role, r, c, source, target, which):
        n = len(relay)
        relay.append((role, r, c, source, target, cand_send.at[n], cand_recv.at[which]))

    mine_v = strip_v.at[edge_v]
    mine_h = strip_h.at[edge_h]
    for far in (0, 1):
        for rev in (0, 1):
            r = 15 - row if rev else row
            c = 7 - col if far else col
            to_relay(is_v, r, c, mine_v, cand_v.at[edge_v * 2 + rev], 0)
    for r in (0, 15):
        for rev in (0, 1):
            c = row // 2
            c = 7 - c if rev else c
            to_relay(is_v, jnp.int32(r), c, mine_v, cand_h.at[edge_v * 2 + rev, row % 2], 1)
    for far in (0, 1):
        for rev in (0, 1):
            r = 15 - row if far else row
            c = 7 - col if rev else col
            to_relay(is_h, r, c, mine_h, cand_h.at[4 + edge_h * 2 + rev], 1)
    for c in (0, 7):
        for rev in (0, 1):
            for b in (0, 1):
                r = 2 * col + b
                r = 15 - r if rev else r
                to_relay(is_h, r, jnp.int32(c), mine_h.at[b], cand_v.at[4 + edge_h * 2 + rev], 0)

    def elsewhere(r, c):
        return jnp.logical_or(r != row, c != col)

    def face_at(step):
        return lax.rem(face + step, 6)

    barrier = pltpu.get_barrier_semaphore()

    def signal(dev):
        pl.semaphore_signal(barrier, inc=1, device_id=dev, device_id_type=MESH)

    def count(condition):
        return jnp.where(condition, 1, 0)

    arrivals = jnp.int32(TILES - 1)
    for condition, dev, *_ in halo:
        pl.when(condition)(functools.partial(signal, dev))
        arrivals += count(condition)
    for role, r, c, *_ in relay:
        condition = jnp.logical_and(role, elsewhere(r, c))
        pl.when(condition)(functools.partial(signal, device(r, c)))
        arrivals += count(condition)
    for role in (is_v, is_h):
        @pl.when(role)
        def _():
            for step in range(1, 6):
                signal((group, face_at(step), tile))
        arrivals += 5 * count(role)

    def owner_at(i):
        y = lax.rem(tile // 8 + i // 8, 8)
        x = lax.rem((tile // 2) % 4 + (i // 2) % 4, 4)
        z = lax.rem(tile % 2 + i % 2, 2)
        return y * 8 + x * 2 + z

    def signal_owner(i, carry):
        signal((group, face, owner_at(i)))
        return carry

    lax.fori_loop(1, TILES, signal_owner, 0)

    wide[:, 256:] = jnp.zeros((CELLS, PAD - 256), F32)
    wide[:, :WIDE] = q_ref[...]
    q = wide[...]
    winds = w_ref[...]
    level = lax.rem(iota((2 * LEV, PAD), 1), LEV)
    inside = iota((2 * LEV, PAD), 1) < WIDE
    spread_u = jnp.where(jnp.logical_and(inside, iota((2 * LEV, PAD), 0) == level), 1.0, 0.0)
    spread_v = jnp.where(jnp.logical_and(inside, iota((2 * LEV, PAD), 0) == level + LEV), 1.0, 0.0)
    u = jnp.dot(winds, spread_u, preferred_element_type=F32, precision=lax.Precision.HIGHEST)
    v = jnp.dot(winds, spread_v, preferred_element_type=F32, precision=lax.Precision.HIGHEST)
    east, west = jnp.maximum(u, 0.0) * q, jnp.minimum(u, 0.0) * q
    north, south = jnp.maximum(v, 0.0) * q, jnp.minimum(v, 0.0) * q
    r8, c8 = iota((ROWS, CELLS), 0), iota((ROWS, CELLS), 1)
    strip_v[0] = dot(onehot(c8 == r8 * COLS), (-west).astype(BF16)).astype(BF16)
    strip_v[1] = dot(onehot(c8 == r8 * COLS + COLS - 1), east.astype(BF16)).astype(BF16)
    for b in (0, 1):
        strip_h[0, b] = (-south[8 * b : 8 * b + 8]).astype(BF16)
        strip_h[1, b] = north[CELLS - 16 + 8 * b : CELLS - 8 + 8 * b].astype(BF16)

    pl.semaphore_wait(barrier, arrivals)

    def copy(source, target, send, recv, dev):
        return pltpu.make_async_remote_copy(
            src_ref=source, dst_ref=target, send_sem=send, recv_sem=recv, device_id=dev, device_id_type=MESH
        )

    for role, r, c, source, target, send, recv in relay:
        @pl.when(jnp.logical_and(role, elsewhere(r, c)))
        def _():
            copy(source, target, send, recv, device(r, c)).start()

        @pl.when(jnp.logical_and(role, jnp.logical_not(elsewhere(r, c))))
        def _():
            pltpu.make_async_copy(source, target, recv).start()

    for condition, dev, source, target, send, recv in halo:
        @pl.when(condition)
        def _():
            copy(source, target, send, recv, dev).start()

    column = iota((CELLS, PAD), 0) % COLS
    zero16 = jnp.zeros((COLS, PAD), F32)
    east_in = jnp.where(column == 0, 0.0, pltpu.roll(east, 1, 0))
    west_in = jnp.where(column == COLS - 1, 0.0, pltpu.roll(west, CELLS - 1, 0))
    north_in = jnp.concatenate([zero16, north[: CELLS - COLS]], axis=0)
    south_in = jnp.concatenate([south[COLS:], zero16], axis=0)
    partial = q - ((east + west_in) - (east_in + west)) - ((north + south_in) - (north_in + south))

    owner_row = owner_ref[...].astype(F32)
    ii, jj = iota((CELLS, CELLS), 0), iota((CELLS, CELLS), 1)
    owner_col = jnp.sum(jnp.where(ii == jj, owner_row, 0.0), axis=1, keepdims=True)
    same = owner_col == owner_row
    rank_col = jnp.sum(jnp.where(jnp.logical_and(same, jj < ii), 1.0, 0.0), axis=1, keepdims=True)
    rank_row = jnp.sum(jnp.where(jnp.logical_and(same, ii < jj), 1.0, 0.0), axis=0, keepdims=True)
    slot_col = owner_col * CAP + rank_col
    slot_row = owner_row * CAP + rank_row
    gather = onehot(iota((SLOTS, CELLS), 0).astype(F32) == slot_row)
    spread = onehot(iota((CELLS, SLOTS), 1).astype(F32) == slot_col)

    def select(edge, length, total):
        pos = iota((length, total), 0)
        cand = iota((length, total), 1)
        parts = []
        for target in range(6):
            source_face, source_edge, rev = (links[target, edge, n] for n in range(3))
            start = (source_edge * 2 + rev) * length + rev * (length - 1)
            start = jnp.where(source_face == face, start, -1000)
            parts.append(onehot(cand == start + (1 - 2 * rev) * pos))
        return jnp.concatenate(parts, axis=0)

    def faces(fwd, rim, send, recv):
        for step in range(1, 6):
            other = face_at(step)
            copy(fwd.at[other], rim.at[face], send.at[step], recv, (group, other, tile)).start()
        pltpu.make_async_copy(fwd.at[face], rim.at[face], recv).start()

    @pl.when(is_v)
    def _():
        pltpu.make_async_copy(cand_v, cand_v, cand_recv.at[0]).wait()
        chosen = dot(select(edge_v, 8, 64), cand_v[...].reshape(64, PAD)).astype(BF16)
        fwd_v[...] = chosen.reshape(6, 8, PAD)
        faces(fwd_v, rim_v, rim_send_v, rim_recv.at[0])

    @pl.when(is_h)
    def _():
        pltpu.make_async_copy(cand_h, cand_h, cand_recv.at[1]).wait()
        chosen = dot(select(2 + edge_h, 16, 128), cand_h[...].reshape(128, PAD)).astype(BF16)
        fwd_h[...] = chosen.reshape(6, 2, 8, PAD)
        faces(fwd_h, rim_h, rim_send_h, rim_recv.at[1])

    for (condition, *_), target, recv in zip(
        halo, (ghost_v.at[0], ghost_v.at[1], ghost_h.at[0], ghost_h.at[1]), (0, 1, 2, 3)
    ):
        @pl.when(condition)
        def _():
            pltpu.make_async_copy(target, target, halo_recv.at[recv]).wait()

    @pl.when(is_v)
    def _():
        pltpu.make_async_copy(rim_v, rim_v, rim_recv.at[0]).wait()
        ghost_v[edge_v] = jnp.sum(rim_v[...].astype(F32), axis=0).astype(BF16)

    @pl.when(is_h)
    def _():
        pltpu.make_async_copy(rim_h, rim_h, rim_recv.at[1]).wait()
        ghost_h[edge_h] = jnp.sum(rim_h[...].astype(F32), axis=0).astype(BF16)

    cell16, pos16 = iota((CELLS, 16), 0), iota((CELLS, 16), 1)
    side = jnp.where(pos16 < 8, pos16 * COLS, (pos16 - 8) * COLS + COLS - 1)
    advected = (
        partial
        + dot(onehot(cell16 == side), ghost_v[...].reshape(16, PAD))
        + dot(onehot(cell16 == pos16), ghost_h[0].reshape(16, PAD))
        + dot(onehot(cell16 == pos16 + CELLS - COLS), ghost_h[1].reshape(16, PAD))
    )
    gap = jnp.zeros((CELLS, FPAD - PAD), F32)
    change = pltpu.roll(jnp.concatenate([advected - q, gap], axis=1), WIDE, 1)
    features = jnp.where(iota((CELLS, FPAD), 1) < WIDE, jnp.concatenate([advected, gap], axis=1), change)
    outbox[...] = dot(gather, features.astype(BF16)).astype(BF16).reshape(TILES, CAP, FPAD)

    def exchange(box, target, send, recv):
        own = pltpu.make_async_copy(box.at[tile], target.at[tile], own_sem)
        own.start()

        def step(i, carry):
            other = owner_at(i)
            copy(box.at[other], target.at[tile], send, recv, (group, face, other)).start()
            return carry

        lax.fori_loop(1, TILES, step, 0)
        own.wait()
        most = target.at[pl.ds(0, TILES - 1)]
        pltpu.make_async_copy(most, most, recv).wait()

    exchange(outbox, inbox, a2a_send, a2a_recv)
    for load in loads:
        load.wait()
    x = inbox[...].reshape(SLOTS, FPAD)[:, :FEAT]
    hidden = silu(dot(x, first[...])).astype(BF16)
    hidden = silu(dot(hidden, middle[...])).astype(BF16)
    reply[:, :, :WIDE] = dot(hidden, last[...]).astype(BF16).reshape(TILES, CAP, WIDE)
    exchange(reply, answers, ret_send, ret_recv)
    tendency = dot(spread, answers[...].reshape(SLOTS, PAD))
    out_ref[...] = (advected + tendency)[:, :WIDE]

    for role, r, c, source, target, send, recv in relay:
        @pl.when(jnp.logical_and(role, elsewhere(r, c)))
        def _():
            copy(source, target, send, recv, device(r, c)).wait_send()
    for condition, dev, source, target, send, recv in halo:
        @pl.when(condition)
        def _():
            copy(source, target, send, recv, dev).wait_send()
    for role, fwd, rim, send in ((is_v, fwd_v, rim_v, rim_send_v), (is_h, fwd_h, rim_h, rim_send_h)):
        @pl.when(role)
        def _():
            for step in range(1, 6):
                other = face_at(step)
                copy(fwd.at[other], rim.at[face], send.at[step], rim_recv.at[0], (group, other, tile)).wait_send()
    most = outbox.at[pl.ds(0, TILES - 1)]
    pltpu.make_async_copy(most, most, a2a_send).wait()
    most = reply.at[pl.ds(0, TILES - 1)]
    pltpu.make_async_copy(most, most, ret_send).wait()


def local(tracers, wind_field, face_links, owner_map, first_layer, middle_layer, last_layer):
    vmem = pl.BlockSpec(memory_space=pltpu.VMEM)
    smem = pl.BlockSpec(memory_space=pltpu.SMEM)
    hbm = pl.BlockSpec(memory_space=pl.ANY)
    dma = pltpu.SemaphoreType.DMA
    updated = pl.pallas_call(
        kernel,
        out_shape=jax.ShapeDtypeStruct((CELLS, WIDE), F32),
        in_specs=[vmem, vmem, smem, vmem, hbm, hbm, hbm],
        out_specs=vmem,
        scratch_shapes=[
            pltpu.VMEM(first_layer.shape[1:], BF16),
            pltpu.VMEM(middle_layer.shape[1:], BF16),
            pltpu.VMEM(last_layer.shape[1:], BF16),
            pltpu.VMEM((2, 8, PAD), BF16),
            pltpu.VMEM((2, 2, 8, PAD), BF16),
            pltpu.VMEM((2, 8, PAD), BF16),
            pltpu.VMEM((2, 2, 8, PAD), BF16),
            pltpu.VMEM((8, 8, PAD), BF16),
            pltpu.VMEM((8, 2, 8, PAD), BF16),
            pltpu.VMEM((6, 8, PAD), BF16),
            pltpu.VMEM((6, 2, 8, PAD), BF16),
            pltpu.VMEM((6, 8, PAD), BF16),
            pltpu.VMEM((6, 2, 8, PAD), BF16),
            pltpu.VMEM((CELLS, PAD), F32),
            pltpu.VMEM((TILES, CAP, FPAD), BF16),
            pltpu.VMEM((TILES, CAP, FPAD), BF16),
            pltpu.VMEM((TILES, CAP, PAD), BF16),
            pltpu.VMEM((TILES, CAP, PAD), BF16),
            dma((3,)),
            dma((4,)),
            dma((4,)),
            dma((20,)),
            dma((2,)),
            dma((6,)),
            dma((6,)),
            dma((2,)),
            dma, dma, dma, dma, dma,
        ],
        compiler_params=pltpu.CompilerParams(collective_id=0, has_side_effects=True),
    )(
        tracers.reshape(CELLS, WIDE),
        wind_field.reshape(CELLS, 2 * LEV),
        face_links,
        owner_map.reshape(1, CELLS),
        first_layer[0],
        middle_layer[0],
        last_layer[0],
    )
    return updated.reshape(tracers.shape)


def solution(mesh):
    in_specs = (
        P("face", ("group", "tile"), None, None, None),
        P("face", ("group", "tile"), None, None, None),
        P(),
        P("face", ("group", "tile"), None, None),
        P("tile", None, None),
        P("tile", None, None),
        P("tile", None, None),
    )
    out_specs = P("face", ("group", "tile"), None, None, None)
    return jax.shard_map(local, mesh=mesh, in_specs=in_specs, out_specs=out_specs, check_vma=False)
```

```python
import functools

import jax
import jax.numpy as jnp
from jax import lax
from jax.experimental import pallas as pl
from jax.experimental.pallas import tpu as pltpu
from jax.sharding import PartitionSpec as P

MESH = pl.DeviceIdType.MESH
ROWS, COLS, LEV = 8, 16, 79
CELLS = ROWS * COLS
WIDE = 4 * LEV
PAD = 384
FEAT = 2 * WIDE
FPAD = 640
TILES = 64
CAP = 4
SLOTS = TILES * CAP
F32, BF16, I32 = jnp.float32, jnp.bfloat16, jnp.int32


def iota(shape, dim):
    return lax.broadcasted_iota(I32, shape, dim)


def onehot(condition):
    return jnp.where(condition, 1.0, 0.0).astype(BF16)


def silu(x):
    return x / (1.0 + jnp.exp(-x))


def dot(a, b):
    return jnp.dot(a, b, preferred_element_type=F32)


def place_of(col):
    lower = col < 4
    return jnp.where(lower, 0, 1), jnp.where(lower, col, 7 - col)


def kernel(
    q_ref, w_ref, links, owner_ref, first_hbm, middle_hbm, last_hbm,
    out_ref,
    first, middle, last,
    strip_v, strip_h, ghost_v, ghost_h,
    cand_v, cand_h, fwd_v, fwd_h, rim_v, rim_h,
    wide, outbox, inbox, reply, answers,
    wsem, halo_send, halo_recv, cand_send, cand_recv, rim_send_v, rim_send_h, rim_recv,
    a2a_send, a2a_recv, ret_send, ret_recv, own_sem, lines,
):
    group, face, tile = (lax.axis_index(a) for a in ("group", "face", "tile"))
    row = tile // 4
    within = tile % 4
    col = jnp.where(group == 0, within, 7 - within)
    is_v = within == 0
    is_n = row == 15
    is_h = jnp.logical_or(row == 0, is_n)
    edge_v = group
    edge_h = jnp.where(is_n, 1, 0)

    loads = [
        pltpu.make_async_copy(first_hbm, first, wsem.at[0]),
        pltpu.make_async_copy(middle_hbm, middle, wsem.at[1]),
        pltpu.make_async_copy(last_hbm, last, wsem.at[2]),
    ]
    for load in loads:
        load.start()

    def device(r, c):
        g, k = place_of(c)
        return (g, face, r * 4 + k)

    halo = [
        (col > 0, device(row, col - 1), strip_v.at[0], ghost_v.at[1], halo_send.at[0], halo_recv.at[1]),
        (col < 7, device(row, col + 1), strip_v.at[1], ghost_v.at[0], halo_send.at[1], halo_recv.at[0]),
        (row > 0, device(row - 1, col), strip_h.at[0], ghost_h.at[1], halo_send.at[2], halo_recv.at[3]),
        (row < 15, device(row + 1, col), strip_h.at[1], ghost_h.at[0], halo_send.at[3], halo_recv.at[2]),
    ]
    relay = []

    def to_relay(role, r, c, source, target, which):
        n = len(relay)
        relay.append((role, r, c, source, target, cand_send.at[n], cand_recv.at[which]))

    mine_v = strip_v.at[edge_v]
    mine_h = strip_h.at[edge_h]
    for far in (0, 1):
        for rev in (0, 1):
            r = 15 - row if rev else row
            c = 7 - col if far else col
            to_relay(is_v, r, c, mine_v, cand_v.at[edge_v * 2 + rev], 0)
    for r in (0, 15):
        for rev in (0, 1):
            c = row // 2
            c = 7 - c if rev else c
            to_relay(is_v, jnp.int32(r), c, mine_v, cand_h.at[edge_v * 2 + rev, row % 2], 1)
    for far in (0, 1):
        for rev in (0, 1):
            r = 15 - row if far else row
            c = 7 - col if rev else col
            to_relay(is_h, r, c, mine_h, cand_h.at[4 + edge_h * 2 + rev], 1)
    for c in (0, 7):
        for rev in (0, 1):
            for b in (0, 1):
                r = 2 * col + b
                r = 15 - r if rev else r
                to_relay(is_h, r, jnp.int32(c), mine_h.at[b], cand_v.at[4 + edge_h * 2 + rev], 0)

    def elsewhere(r, c):
        return jnp.logical_or(r != row, c != col)

    def face_at(step):
        return lax.rem(face + step, 6)

    barrier = pltpu.get_barrier_semaphore()

    def signal(dev):
        pl.semaphore_signal(barrier, inc=1, device_id=dev, device_id_type=MESH)

    def count(condition):
        return jnp.where(condition, 1, 0)

    arrivals = jnp.int32(14)
    for condition, dev, *_ in halo:
        pl.when(condition)(functools.partial(signal, dev))
        arrivals += count(condition)
    for role, r, c, *_ in relay:
        condition = jnp.logical_and(role, elsewhere(r, c))
        pl.when(condition)(functools.partial(signal, device(r, c)))
        arrivals += count(condition)
    for role in (is_v, is_h):
        @pl.when(role)
        def _():
            for step in range(1, 6):
                signal((group, face_at(step), tile))
        arrivals += 5 * count(role)

    def owner_at(i):
        y = lax.rem(tile // 8 + i // 8, 8)
        x = lax.rem((tile // 2) % 4 + (i // 2) % 4, 4)
        z = lax.rem(tile % 2 + i % 2, 2)
        return y * 8 + x * 2 + z

    for i in range(1, 8):
        signal((group, face, owner_at(i)))
        signal((group, face, owner_at(8 * i)))

    wide[:, 256:] = jnp.zeros((CELLS, PAD - 256), F32)
    wide[:, :WIDE] = q_ref[...]
    q = wide[...]
    winds = w_ref[...]
    level = lax.rem(iota((2 * LEV, PAD), 1), LEV)
    inside = iota((2 * LEV, PAD), 1) < WIDE
    spread_u = jnp.where(jnp.logical_and(inside, iota((2 * LEV, PAD), 0) == level), 1.0, 0.0)
    spread_v = jnp.where(jnp.logical_and(inside, iota((2 * LEV, PAD), 0) == level + LEV), 1.0, 0.0)
    u = jnp.dot(winds, spread_u, preferred_element_type=F32, precision=lax.Precision.HIGHEST)
    v = jnp.dot(winds, spread_v, preferred_element_type=F32, precision=lax.Precision.HIGHEST)
    east, west = jnp.maximum(u, 0.0) * q, jnp.minimum(u, 0.0) * q
    north, south = jnp.maximum(v, 0.0) * q, jnp.minimum(v, 0.0) * q
    r8, c8 = iota((ROWS, CELLS), 0), iota((ROWS, CELLS), 1)
    strip_v[0] = dot(onehot(c8 == r8 * COLS), (-west).astype(BF16)).astype(BF16)
    strip_v[1] = dot(onehot(c8 == r8 * COLS + COLS - 1), east.astype(BF16)).astype(BF16)
    for b in (0, 1):
        strip_h[0, b] = (-south[8 * b : 8 * b + 8]).astype(BF16)
        strip_h[1, b] = north[CELLS - 16 + 8 * b : CELLS - 8 + 8 * b].astype(BF16)

    pl.semaphore_wait(barrier, arrivals)
    for i in range(1, 8):
        pl.semaphore_signal(lines, inc=1, device_id=(group, face, owner_at(8 * i)), device_id_type=MESH)

    def copy(source, target, send, recv, dev):
        return pltpu.make_async_remote_copy(
            src_ref=source, dst_ref=target, send_sem=send, recv_sem=recv, device_id=dev, device_id_type=MESH
        )

    for role, r, c, source, target, send, recv in relay:
        @pl.when(jnp.logical_and(role, elsewhere(r, c)))
        def _():
            copy(source, target, send, recv, device(r, c)).start()

        @pl.when(jnp.logical_and(role, jnp.logical_not(elsewhere(r, c))))
        def _():
            pltpu.make_async_copy(source, target, recv).start()

    for condition, dev, source, target, send, recv in halo:
        @pl.when(condition)
        def _():
            copy(source, target, send, recv, dev).start()

    column = iota((CELLS, PAD), 0) % COLS
    zero16 = jnp.zeros((COLS, PAD), F32)
    east_in = jnp.where(column == 0, 0.0, pltpu.roll(east, 1, 0))
    west_in = jnp.where(column == COLS - 1, 0.0, pltpu.roll(west, CELLS - 1, 0))
    north_in = jnp.concatenate([zero16, north[: CELLS - COLS]], axis=0)
    south_in = jnp.concatenate([south[COLS:], zero16], axis=0)
    partial = q - ((east + west_in) - (east_in + west)) - ((north + south_in) - (north_in + south))

    owner_row = owner_ref[...].astype(F32)
    ii, jj = iota((CELLS, CELLS), 0), iota((CELLS, CELLS), 1)
    owner_col = jnp.sum(jnp.where(ii == jj, owner_row, 0.0), axis=1, keepdims=True)
    same = owner_col == owner_row
    rank_col = jnp.sum(jnp.where(jnp.logical_and(same, jj < ii), 1.0, 0.0), axis=1, keepdims=True)
    rank_row = jnp.sum(jnp.where(jnp.logical_and(same, ii < jj), 1.0, 0.0), axis=0, keepdims=True)
    slot_col = owner_col * CAP + rank_col
    slot_row = owner_row * CAP + rank_row
    gather = onehot(iota((SLOTS, CELLS), 0).astype(F32) == slot_row)
    spread = onehot(iota((CELLS, SLOTS), 1).astype(F32) == slot_col)

    def select(edge, length, total):
        pos = iota((length, total), 0)
        cand = iota((length, total), 1)
        parts = []
        for target in range(6):
            source_face, source_edge, rev = (links[n, edge, target] for n in range(3))
            start = (source_edge * 2 + rev) * length + rev * (length - 1)
            start = jnp.where(source_face == face, start, -1000)
            parts.append(onehot(cand == start + (1 - 2 * rev) * pos))
        return jnp.concatenate(parts, axis=0)

    def faces(fwd, rim, send, recv):
        for step in range(1, 6):
            other = face_at(step)
            copy(fwd.at[other], rim.at[face], send.at[step], recv, (group, other, tile)).start()
        pltpu.make_async_copy(fwd.at[face], rim.at[face], recv).start()

    @pl.when(is_v)
    def _():
        pltpu.make_async_copy(cand_v, cand_v, cand_recv.at[0]).wait()
        chosen = dot(select(edge_v, 8, 64), cand_v[...].reshape(64, PAD)).astype(BF16)
        fwd_v[...] = chosen.reshape(6, 8, PAD)
        faces(fwd_v, rim_v, rim_send_v, rim_recv.at[0])

    @pl.when(is_h)
    def _():
        pltpu.make_async_copy(cand_h, cand_h, cand_recv.at[1]).wait()
        chosen = dot(select(2 + edge_h, 16, 128), cand_h[...].reshape(128, PAD)).astype(BF16)
        fwd_h[...] = chosen.reshape(6, 2, 8, PAD)
        faces(fwd_h, rim_h, rim_send_h, rim_recv.at[1])

    for (condition, *_), target, recv in zip(
        halo, (ghost_v.at[0], ghost_v.at[1], ghost_h.at[0], ghost_h.at[1]), (0, 1, 2, 3)
    ):
        @pl.when(condition)
        def _():
            pltpu.make_async_copy(target, target, halo_recv.at[recv]).wait()

    @pl.when(is_v)
    def _():
        pltpu.make_async_copy(rim_v, rim_v, rim_recv.at[0]).wait()
        ghost_v[edge_v] = jnp.sum(rim_v[...].astype(F32), axis=0).astype(BF16)

    @pl.when(is_h)
    def _():
        pltpu.make_async_copy(rim_h, rim_h, rim_recv.at[1]).wait()
        ghost_h[edge_h] = jnp.sum(rim_h[...].astype(F32), axis=0).astype(BF16)

    cell16, pos16 = iota((CELLS, 16), 0), iota((CELLS, 16), 1)
    side = jnp.where(pos16 < 8, pos16 * COLS, (pos16 - 8) * COLS + COLS - 1)
    advected = (
        partial
        + dot(onehot(cell16 == side), ghost_v[...].reshape(16, PAD))
        + dot(onehot(cell16 == pos16), ghost_h[0].reshape(16, PAD))
        + dot(onehot(cell16 == pos16 + CELLS - COLS), ghost_h[1].reshape(16, PAD))
    )
    gap = jnp.zeros((CELLS, FPAD - PAD), F32)
    change = pltpu.roll(jnp.concatenate([advected - q, gap], axis=1), WIDE, 1)
    features = jnp.where(iota((CELLS, FPAD), 1) < WIDE, jnp.concatenate([advected, gap], axis=1), change)
    outbox[...] = dot(gather, features.astype(BF16)).astype(BF16).reshape(TILES, CAP, FPAD)

    def exchange(box, target, send, recv):
        own = pltpu.make_async_copy(box.at[tile], target.at[tile], own_sem)
        own.start()

        def step(i, carry):
            other = owner_at(i)
            copy(box.at[other], target.at[tile], send, recv, (group, face, other)).start()
            return carry

        lax.fori_loop(1, TILES, step, 0)
        own.wait()
        most = target.at[pl.ds(0, TILES - 1)]
        pltpu.make_async_copy(most, most, recv).wait()

    pl.semaphore_wait(lines, 7)
    exchange(outbox, inbox, a2a_send, a2a_recv)
    for load in loads:
        load.wait()
    x = inbox[...].reshape(SLOTS, FPAD)[:, :FEAT]
    hidden = silu(dot(x, first[...])).astype(BF16)
    hidden = silu(dot(hidden, middle[...])).astype(BF16)
    out = lax.dot_general(hidden, last[...], (((1,), (1,)), ((), ())), preferred_element_type=F32)
    reply[:, :, :WIDE] = out.astype(BF16).reshape(TILES, CAP, WIDE)
    exchange(reply, answers, ret_send, ret_recv)
    tendency = dot(spread, answers[...].reshape(SLOTS, PAD))
    out_ref[...] = (advected + tendency)[:, :WIDE]

    for role, r, c, source, target, send, recv in relay:
        @pl.when(jnp.logical_and(role, elsewhere(r, c)))
        def _():
            copy(source, target, send, recv, device(r, c)).wait_send()
    for condition, dev, source, target, send, recv in halo:
        @pl.when(condition)
        def _():
            copy(source, target, send, recv, dev).wait_send()
    for role, fwd, rim, send in ((is_v, fwd_v, rim_v, rim_send_v), (is_h, fwd_h, rim_h, rim_send_h)):
        @pl.when(role)
        def _():
            for step in range(1, 6):
                other = face_at(step)
                copy(fwd.at[other], rim.at[face], send.at[step], rim_recv.at[0], (group, other, tile)).wait_send()
    most = outbox.at[pl.ds(0, TILES - 1)]
    pltpu.make_async_copy(most, most, a2a_send).wait()
    most = reply.at[pl.ds(0, TILES - 1)]
    pltpu.make_async_copy(most, most, ret_send).wait()


def local(tracers, wind_field, face_links, owner_map, first_layer, middle_layer, last_layer):
    vmem = pl.BlockSpec(memory_space=pltpu.VMEM)
    smem = pl.BlockSpec(memory_space=pltpu.SMEM)
    hbm = pl.BlockSpec(memory_space=pl.ANY)
    dma = pltpu.SemaphoreType.DMA
    updated = pl.pallas_call(
        kernel,
        out_shape=jax.ShapeDtypeStruct((CELLS, WIDE), F32),
        in_specs=[vmem, vmem, smem, vmem, hbm, hbm, hbm],
        out_specs=vmem,
        scratch_shapes=[
            pltpu.VMEM(first_layer.shape[1:], BF16),
            pltpu.VMEM(middle_layer.shape[1:], BF16),
            pltpu.VMEM(last_layer.shape[:0:-1], BF16),
            pltpu.VMEM((2, 8, PAD), BF16),
            pltpu.VMEM((2, 2, 8, PAD), BF16),
            pltpu.VMEM((2, 8, PAD), BF16),
            pltpu.VMEM((2, 2, 8, PAD), BF16),
            pltpu.VMEM((8, 8, PAD), BF16),
            pltpu.VMEM((8, 2, 8, PAD), BF16),
            pltpu.VMEM((6, 8, PAD), BF16),
            pltpu.VMEM((6, 2, 8, PAD), BF16),
            pltpu.VMEM((6, 8, PAD), BF16),
            pltpu.VMEM((6, 2, 8, PAD), BF16),
            pltpu.VMEM((CELLS, PAD), F32),
            pltpu.VMEM((TILES, CAP, FPAD), BF16),
            pltpu.VMEM((TILES, CAP, FPAD), BF16),
            pltpu.VMEM((TILES, CAP, PAD), BF16),
            pltpu.VMEM((TILES, CAP, PAD), BF16),
            dma((3,)),
            dma((4,)),
            dma((4,)),
            dma((20,)),
            dma((2,)),
            dma((6,)),
            dma((6,)),
            dma((2,)),
            dma, dma, dma, dma, dma,
            pltpu.SemaphoreType.REGULAR,
        ],
        compiler_params=pltpu.CompilerParams(collective_id=0, has_side_effects=True),
    )(
        tracers.reshape(CELLS, WIDE),
        wind_field.reshape(CELLS, 2 * LEV),
        face_links.transpose(2, 1, 0),
        owner_map.reshape(1, CELLS),
        first_layer[0],
        middle_layer[0],
        last_layer[0].T,
    )
    return updated.reshape(tracers.shape)


def solution(mesh):
    in_specs = (
        P("face", ("group", "tile"), None, None, None),
        P("face", ("group", "tile"), None, None, None),
        P(),
        P("face", ("group", "tile"), None, None),
        P("tile", None, None),
        P("tile", None, None),
        P("tile", None, None),
    )
    out_specs = P("face", ("group", "tile"), None, None, None)
    return jax.shard_map(local, mesh=mesh, in_specs=in_specs, out_specs=out_specs, check_vma=False)
```

```python
import functools

import jax
import jax.numpy as jnp
from jax import lax
from jax.experimental import pallas as pl
from jax.experimental.pallas import tpu as pltpu
from jax.sharding import PartitionSpec as P

MESH = pl.DeviceIdType.MESH
ROWS, COLS, LEV = 8, 16, 79
CELLS = ROWS * COLS
WIDE = 4 * LEV
PAD = 384
FEAT = 2 * WIDE
FPAD = 640
TILES = 64
CAP = 4
SLOTS = TILES * CAP
F32, BF16, I32 = jnp.float32, jnp.bfloat16, jnp.int32


def iota(shape, dim):
    return lax.broadcasted_iota(I32, shape, dim)


def onehot(condition):
    return jnp.where(condition, 1.0, 0.0).astype(BF16)


def silu(x):
    return x / (1.0 + jnp.exp(-x))


def dot(a, b):
    return jnp.dot(a, b, preferred_element_type=F32)


def place_of(col):
    lower = col < 4
    return jnp.where(lower, 0, 1), jnp.where(lower, col, 7 - col)


def kernel(
    q_ref, w_ref, links, owner_ref, first_hbm, middle_hbm, last_hbm,
    out_ref,
    first, middle, last,
    strip_v, strip_h, ghost_v, ghost_h,
    cand_v, cand_h, fwd_v, fwd_h, rim_v, rim_h,
    wide, outbox, inbox, reply, answers,
    wsem, halo_send, halo_recv, cand_send, cand_recv, rim_send_v, rim_send_h, rim_recv,
    a2a_send, a2a_recv, ret_send, ret_recv, lines,
):
    group, face, tile = (lax.axis_index(a) for a in ("group", "face", "tile"))
    row = tile // 4
    within = tile % 4
    col = jnp.where(group == 0, within, 7 - within)
    is_v = within == 0
    is_n = row == 15
    is_h = jnp.logical_or(row == 0, is_n)
    edge_v = group
    edge_h = jnp.where(is_n, 1, 0)

    tile_y, tile_x, half = tile // 8, (tile // 2) % 4, tile % 2
    pair_depth = lax.rem(6 * half + face + jnp.where(face < 3, 9, 3), 12)
    pair_half, pair_face = pair_depth // 6, pair_depth % 6
    weights = ((first_hbm, first, 0), (middle_hbm, middle, 1), (last_hbm, last, 2))
    for source, target, n in weights:
        pltpu.make_async_copy(source, target, wsem.at[n]).start()

    def device(r, c):
        g, k = place_of(c)
        return (g, face, r * 4 + k)

    halo = [
        (col > 0, device(row, col - 1), strip_v.at[0], ghost_v.at[1], halo_send.at[0], halo_recv.at[1]),
        (col < 7, device(row, col + 1), strip_v.at[1], ghost_v.at[0], halo_send.at[1], halo_recv.at[0]),
        (row > 0, device(row - 1, col), strip_h.at[0], ghost_h.at[1], halo_send.at[2], halo_recv.at[3]),
        (row < 15, device(row + 1, col), strip_h.at[1], ghost_h.at[0], halo_send.at[3], halo_recv.at[2]),
    ]
    relay = []

    def to_relay(role, r, c, source, target, which):
        n = len(relay)
        relay.append((role, r, c, source, target, cand_send.at[n], cand_recv.at[which]))

    mine_v = strip_v.at[edge_v]
    mine_h = strip_h.at[edge_h]
    for far in (0, 1):
        for rev in (0, 1):
            r = 15 - row if rev else row
            c = 7 - col if far else col
            to_relay(is_v, r, c, mine_v, cand_v.at[edge_v * 2 + rev], 0)
    for r in (0, 15):
        for rev in (0, 1):
            c = row // 2
            c = 7 - c if rev else c
            to_relay(is_v, jnp.int32(r), c, mine_v, cand_h.at[edge_v * 2 + rev, row % 2], 1)
    for far in (0, 1):
        for rev in (0, 1):
            r = 15 - row if far else row
            c = 7 - col if rev else col
            to_relay(is_h, r, c, mine_h, cand_h.at[4 + edge_h * 2 + rev], 1)
    for c in (0, 7):
        for rev in (0, 1):
            for b in (0, 1):
                r = 2 * col + b
                r = 15 - r if rev else r
                to_relay(is_h, r, jnp.int32(c), mine_h.at[b], cand_v.at[4 + edge_h * 2 + rev], 0)

    def elsewhere(r, c):
        return jnp.logical_or(r != row, c != col)

    def face_at(step):
        return lax.rem(face + step, 6)

    barrier = pltpu.get_barrier_semaphore()

    def signal(dev):
        pl.semaphore_signal(barrier, inc=1, device_id=dev, device_id_type=MESH)

    def count(condition):
        return jnp.where(condition, 1, 0)

    arrivals = jnp.int32(0)
    for condition, dev, *_ in halo:
        pl.when(condition)(functools.partial(signal, dev))
        arrivals += count(condition)
    for role, r, c, *_ in relay:
        condition = jnp.logical_and(role, elsewhere(r, c))
        pl.when(condition)(functools.partial(signal, device(r, c)))
        arrivals += count(condition)
    for role in (is_v, is_h):
        @pl.when(role)
        def _():
            for step in range(1, 6):
                signal((group, face_at(step), tile))
        arrivals += 5 * count(role)

    def at(partner, y, x):
        f, z = jnp.where(partner == 1, pair_face, face), jnp.where(partner == 1, pair_half, half)
        return (group, f, lax.rem(tile_y + y, 8) * 8 + lax.rem(tile_x + x, 4) * 2 + z)

    for x in range(1, 4):
        signal(at(0, 0, x))
    for y in range(1, 8):
        signal(at(0, y, 0))
    signal(at(1, 0, 0))
    arrivals += 11

    wide[:, 256:] = jnp.zeros((CELLS, PAD - 256), F32)
    wide[:, :WIDE] = q_ref[...]
    q = wide[...]
    winds = w_ref[...]
    level = lax.rem(iota((2 * LEV, PAD), 1), LEV)
    inside = iota((2 * LEV, PAD), 1) < WIDE
    spread_u = jnp.where(jnp.logical_and(inside, iota((2 * LEV, PAD), 0) == level), 1.0, 0.0)
    spread_v = jnp.where(jnp.logical_and(inside, iota((2 * LEV, PAD), 0) == level + LEV), 1.0, 0.0)
    u = jnp.dot(winds, spread_u, preferred_element_type=F32, precision=lax.Precision.HIGHEST)
    v = jnp.dot(winds, spread_v, preferred_element_type=F32, precision=lax.Precision.HIGHEST)
    east, west = jnp.maximum(u, 0.0) * q, jnp.minimum(u, 0.0) * q
    north, south = jnp.maximum(v, 0.0) * q, jnp.minimum(v, 0.0) * q
    r8, c8 = iota((ROWS, CELLS), 0), iota((ROWS, CELLS), 1)
    strip_v[0] = dot(onehot(c8 == r8 * COLS), (-west).astype(BF16)).astype(BF16)
    strip_v[1] = dot(onehot(c8 == r8 * COLS + COLS - 1), east.astype(BF16)).astype(BF16)
    for b in (0, 1):
        strip_h[0, b] = (-south[8 * b : 8 * b + 8]).astype(BF16)
        strip_h[1, b] = north[CELLS - 16 + 8 * b : CELLS - 8 + 8 * b].astype(BF16)

    pl.semaphore_wait(barrier, arrivals)
    for x in range(1, 4):
        pl.semaphore_signal(lines.at[0], inc=1, device_id=at(0, 0, x), device_id_type=MESH)

    def copy(source, target, send, recv, dev):
        return pltpu.make_async_remote_copy(
            src_ref=source, dst_ref=target, send_sem=send, recv_sem=recv, device_id=dev, device_id_type=MESH
        )

    for role, r, c, source, target, send, recv in relay:
        @pl.when(jnp.logical_and(role, elsewhere(r, c)))
        def _():
            copy(source, target, send, recv, device(r, c)).start()

        @pl.when(jnp.logical_and(role, jnp.logical_not(elsewhere(r, c))))
        def _():
            pltpu.make_async_copy(source, target, recv).start()

    for condition, dev, source, target, send, recv in halo:
        @pl.when(condition)
        def _():
            copy(source, target, send, recv, dev).start()

    column = iota((CELLS, PAD), 0) % COLS
    zero16 = jnp.zeros((COLS, PAD), F32)
    east_in = jnp.where(column == 0, 0.0, pltpu.roll(east, 1, 0))
    west_in = jnp.where(column == COLS - 1, 0.0, pltpu.roll(west, CELLS - 1, 0))
    north_in = jnp.concatenate([zero16, north[: CELLS - COLS]], axis=0)
    south_in = jnp.concatenate([south[COLS:], zero16], axis=0)
    partial = q - ((east + west_in) - (east_in + west)) - ((north + south_in) - (north_in + south))

    owner_row = owner_ref[...].astype(F32)
    ii, jj = iota((CELLS, CELLS), 0), iota((CELLS, CELLS), 1)
    owner_col = jnp.sum(jnp.where(ii == jj, owner_row, 0.0), axis=1, keepdims=True)
    same = owner_col == owner_row
    rank_col = jnp.sum(jnp.where(jnp.logical_and(same, jj < ii), 1.0, 0.0), axis=1, keepdims=True)
    rank_row = jnp.sum(jnp.where(jnp.logical_and(same, ii < jj), 1.0, 0.0), axis=0, keepdims=True)
    slot_col = owner_col * CAP + rank_col
    slot_row = owner_row * CAP + rank_row
    gather = onehot(iota((SLOTS, CELLS), 0).astype(F32) == slot_row)
    spread = onehot(iota((CELLS, SLOTS), 1).astype(F32) == slot_col)

    pl.semaphore_wait(lines.at[0], 3)
    for y in range(1, 8):
        pl.semaphore_signal(lines.at[1], inc=1, device_id=at(0, y, 0), device_id_type=MESH)

    def select(edge, length, total):
        pos = iota((length, total), 0)
        cand = iota((length, total), 1)
        parts = []
        for target in range(6):
            source_face, source_edge, rev = (links[n, edge, target] for n in range(3))
            start = (source_edge * 2 + rev) * length + rev * (length - 1)
            start = jnp.where(source_face == face, start, -1000)
            parts.append(onehot(cand == start + (1 - 2 * rev) * pos))
        return jnp.concatenate(parts, axis=0)

    def faces(fwd, rim, send, recv):
        for step in range(1, 6):
            other = face_at(step)
            copy(fwd.at[other], rim.at[face], send.at[step], recv, (group, other, tile)).start()
        pltpu.make_async_copy(fwd.at[face], rim.at[face], recv).start()

    @pl.when(is_v)
    def _():
        pltpu.make_async_copy(cand_v, cand_v, cand_recv.at[0]).wait()
        chosen = dot(select(edge_v, 8, 64), cand_v[...].reshape(64, PAD)).astype(BF16)
        fwd_v[...] = chosen.reshape(6, 8, PAD)
        faces(fwd_v, rim_v, rim_send_v, rim_recv.at[0])

    @pl.when(is_h)
    def _():
        pltpu.make_async_copy(cand_h, cand_h, cand_recv.at[1]).wait()
        chosen = dot(select(2 + edge_h, 16, 128), cand_h[...].reshape(128, PAD)).astype(BF16)
        fwd_h[...] = chosen.reshape(6, 2, 8, PAD)
        faces(fwd_h, rim_h, rim_send_h, rim_recv.at[1])

    for (condition, *_), target, recv in zip(
        halo, (ghost_v.at[0], ghost_v.at[1], ghost_h.at[0], ghost_h.at[1]), (0, 1, 2, 3)
    ):
        @pl.when(condition)
        def _():
            pltpu.make_async_copy(target, target, halo_recv.at[recv]).wait()

    @pl.when(is_v)
    def _():
        pltpu.make_async_copy(rim_v, rim_v, rim_recv.at[0]).wait()
        ghost_v[edge_v] = jnp.sum(rim_v[...].astype(F32), axis=0).astype(BF16)

    @pl.when(is_h)
    def _():
        pltpu.make_async_copy(rim_h, rim_h, rim_recv.at[1]).wait()
        ghost_h[edge_h] = jnp.sum(rim_h[...].astype(F32), axis=0).astype(BF16)

    cell16, pos16 = iota((CELLS, 16), 0), iota((CELLS, 16), 1)
    side = jnp.where(pos16 < 8, pos16 * COLS, (pos16 - 8) * COLS + COLS - 1)
    advected = (
        partial
        + dot(onehot(cell16 == side), ghost_v[...].reshape(16, PAD))
        + dot(onehot(cell16 == pos16), ghost_h[0].reshape(16, PAD))
        + dot(onehot(cell16 == pos16 + CELLS - COLS), ghost_h[1].reshape(16, PAD))
    )
    gap = jnp.zeros((CELLS, FPAD - PAD), F32)
    change = pltpu.roll(jnp.concatenate([advected - q, gap], axis=1), WIDE, 1)
    features = jnp.where(iota((CELLS, FPAD), 1) < WIDE, jnp.concatenate([advected, gap], axis=1), change)
    outbox[...] = dot(gather, features.astype(BF16)).astype(BF16).reshape(TILES, CAP, FPAD)

    chip = tile_y * 4 + tile_x
    pl.semaphore_wait(lines.at[1], 7)

    def exchange(box, target, box_index, target_index, send, recv):
        def remote(y, x, partner):
            dev = at(partner, y, x)
            there = dev[2] // 2
            return copy(box.at[box_index(there, partner)], target.at[target_index(partner)], send, recv, dev)

        def step(i, carry):
            remote(1 + i // 8, (i // 2) % 4, 1 - i % 2).start()
            return carry

        lax.fori_loop(0, 57, step, 0)
        lax.fori_loop(58, TILES, step, 0)
        pltpu.make_async_copy(box.at[box_index(chip, 0)], target.at[target_index(0)], recv).start()
        pltpu.make_async_copy(target, target, recv).wait()

    def expert(there, partner):
        return there * 2 + jnp.where(partner == 1, 1 - half, half)

    def block(there, partner):
        return partner * 32 + there

    exchange(outbox, inbox, expert, lambda partner: block(chip, partner), a2a_send, a2a_recv)
    for source, target, n in weights:
        pltpu.make_async_copy(source, target, wsem.at[n]).wait()
    x = inbox[...].reshape(SLOTS, FPAD)[:, :FEAT]
    hidden = silu(dot(x, first[...])).astype(BF16)
    hidden = silu(dot(hidden, middle[...])).astype(BF16)
    out = lax.dot_general(hidden, last[...], (((1,), (1,)), ((), ())), preferred_element_type=F32)
    reply[:, :, :WIDE] = out.astype(BF16).reshape(TILES, CAP, WIDE)
    exchange(reply, answers, block, lambda partner: expert(chip, 0), ret_send, ret_recv)
    tendency = dot(spread, answers[...].reshape(SLOTS, PAD))
    out_ref[...] = (advected + tendency)[:, :WIDE]

    for role, r, c, source, target, send, recv in relay:
        @pl.when(jnp.logical_and(role, elsewhere(r, c)))
        def _():
            copy(source, target, send, recv, device(r, c)).wait_send()
    for condition, dev, source, target, send, recv in halo:
        @pl.when(condition)
        def _():
            copy(source, target, send, recv, dev).wait_send()
    for role, fwd, rim, send in ((is_v, fwd_v, rim_v, rim_send_v), (is_h, fwd_h, rim_h, rim_send_h)):
        @pl.when(role)
        def _():
            for step in range(1, 6):
                other = face_at(step)
                copy(fwd.at[other], rim.at[face], send.at[step], rim_recv.at[0], (group, other, tile)).wait_send()
    for box, send in ((outbox, a2a_send), (reply, ret_send)):
        most = box.at[pl.ds(0, TILES - 1)]
        pltpu.make_async_copy(most, most, send).wait()


def local(tracers, wind_field, face_links, owner_map, first_layer, middle_layer, last_layer):
    vmem = pl.BlockSpec(memory_space=pltpu.VMEM)
    smem = pl.BlockSpec(memory_space=pltpu.SMEM)
    hbm = pl.BlockSpec(memory_space=pl.ANY)
    dma = pltpu.SemaphoreType.DMA
    updated = pl.pallas_call(
        kernel,
        out_shape=jax.ShapeDtypeStruct((CELLS, WIDE), F32),
        in_specs=[vmem, vmem, smem, vmem, hbm, hbm, hbm],
        out_specs=vmem,
        scratch_shapes=[
            pltpu.VMEM(first_layer.shape[1:], BF16),
            pltpu.VMEM(middle_layer.shape[1:], BF16),
            pltpu.VMEM(last_layer.shape[:0:-1], BF16),
            pltpu.VMEM((2, 8, PAD), BF16),
            pltpu.VMEM((2, 2, 8, PAD), BF16),
            pltpu.VMEM((2, 8, PAD), BF16),
            pltpu.VMEM((2, 2, 8, PAD), BF16),
            pltpu.VMEM((8, 8, PAD), BF16),
            pltpu.VMEM((8, 2, 8, PAD), BF16),
            pltpu.VMEM((6, 8, PAD), BF16),
            pltpu.VMEM((6, 2, 8, PAD), BF16),
            pltpu.VMEM((6, 8, PAD), BF16),
            pltpu.VMEM((6, 2, 8, PAD), BF16),
            pltpu.VMEM((CELLS, PAD), F32),
            pltpu.VMEM((TILES, CAP, FPAD), BF16),
            pltpu.VMEM((TILES, CAP, FPAD), BF16),
            pltpu.VMEM((TILES, CAP, PAD), BF16),
            pltpu.VMEM((TILES, CAP, PAD), BF16),
            dma((3,)),
            dma((4,)),
            dma((4,)),
            dma((20,)),
            dma((2,)),
            dma((6,)),
            dma((6,)),
            dma((2,)),
            dma, dma, dma, dma,
            pltpu.SemaphoreType.REGULAR((2,)),
        ],
        compiler_params=pltpu.CompilerParams(collective_id=0, has_side_effects=True),
    )(
        tracers.reshape(CELLS, WIDE),
        wind_field.reshape(CELLS, 2 * LEV),
        face_links.transpose(2, 1, 0),
        owner_map.reshape(1, CELLS),
        first_layer[0],
        middle_layer[0],
        last_layer[0].T,
    )
    return updated.reshape(tracers.shape)


def solution(mesh):
    in_specs = (
        P("face", ("group", "tile"), None, None, None),
        P("face", ("group", "tile"), None, None, None),
        P(),
        P("face", ("group", "tile"), None, None),
        P("tile", None, None),
        P("tile", None, None),
        P("tile", None, None),
    )
    out_specs = P("face", ("group", "tile"), None, None, None)
    return jax.shard_map(local, mesh=mesh, in_specs=in_specs, out_specs=out_specs, check_vma=False)
```

```python
import functools

import jax
import jax.numpy as jnp
from jax import lax
from jax.experimental import pallas as pl
from jax.experimental.pallas import tpu as pltpu
from jax.sharding import PartitionSpec as P

MESH = pl.DeviceIdType.MESH
ROWS, COLS, LEV = 8, 16, 79
CELLS = ROWS * COLS
WIDE = 4 * LEV
PAD = 384
FEAT = 2 * WIDE
FPAD = 640
TILES = 64
CAP = 4
SLOTS = TILES * CAP
F32, BF16, I32 = jnp.float32, jnp.bfloat16, jnp.int32


def iota(shape, dim):
    return lax.broadcasted_iota(I32, shape, dim)


def onehot(condition):
    return jnp.where(condition, 1.0, 0.0).astype(BF16)


def silu(x):
    return x / (1.0 + jnp.exp(-x))


def dot(a, b):
    return jnp.dot(a, b, preferred_element_type=F32)


def place_of(col):
    lower = col < 4
    return jnp.where(lower, 0, 1), jnp.where(lower, col, 7 - col)


def kernel(
    q_ref, w_ref, links, owner_ref, first_hbm, middle_hbm, last_hbm,
    out_ref,
    first, middle, last,
    strip_v, strip_h, ghost_v, ghost_h,
    cand_v, cand_h, fwd_v, fwd_h, rim_v, rim_h,
    wide, spread_winds, outbox, inbox, reply, answers,
    wsem, halo_send, halo_recv, cand_send, cand_recv, rim_send_v, rim_send_h, rim_recv,
    a2a_send, a2a_recv, ret_send, ret_recv, lines,
):
    group, face, tile = (lax.axis_index(a) for a in ("group", "face", "tile"))
    row = tile // 4
    within = tile % 4
    col = jnp.where(group == 0, within, 7 - within)
    is_v = within == 0
    is_n = row == 15
    is_h = jnp.logical_or(row == 0, is_n)
    edge_v = group
    edge_h = jnp.where(is_n, 1, 0)

    tile_y, tile_x, half = tile // 8, (tile // 2) % 4, tile % 2
    pair_depth = lax.rem(6 * half + face + jnp.where(face < 3, 9, 3), 12)
    pair_half, pair_face = pair_depth // 6, pair_depth % 6
    weights = ((first_hbm, first, 0), (middle_hbm, middle, 1), (last_hbm, last, 2))
    for source, target, n in weights:
        pltpu.make_async_copy(source, target, wsem.at[n]).start()

    def device(r, c):
        g, k = place_of(c)
        return (g, face, r * 4 + k)

    halo = [
        (col > 0, device(row, col - 1), strip_v.at[0], ghost_v.at[1], halo_send.at[0], halo_recv.at[1]),
        (col < 7, device(row, col + 1), strip_v.at[1], ghost_v.at[0], halo_send.at[1], halo_recv.at[0]),
        (row > 0, device(row - 1, col), strip_h.at[0], ghost_h.at[1], halo_send.at[2], halo_recv.at[3]),
        (row < 15, device(row + 1, col), strip_h.at[1], ghost_h.at[0], halo_send.at[3], halo_recv.at[2]),
    ]
    relay = []

    def to_relay(role, r, c, source, target, which):
        n = len(relay)
        relay.append((role, r, c, source, target, cand_send.at[n], cand_recv.at[which]))

    mine_v = strip_v.at[edge_v]
    mine_h = strip_h.at[edge_h]
    for far in (0, 1):
        for rev in (0, 1):
            r = 15 - row if rev else row
            c = 7 - col if far else col
            to_relay(is_v, r, c, mine_v, cand_v.at[edge_v * 2 + rev], 0)
    for r in (0, 15):
        for rev in (0, 1):
            c = row // 2
            c = 7 - c if rev else c
            to_relay(is_v, jnp.int32(r), c, mine_v, cand_h.at[edge_v * 2 + rev, row % 2], 1)
    for far in (0, 1):
        for rev in (0, 1):
            r = 15 - row if far else row
            c = 7 - col if rev else col
            to_relay(is_h, r, c, mine_h, cand_h.at[4 + edge_h * 2 + rev], 1)
    for c in (0, 7):
        for rev in (0, 1):
            for b in (0, 1):
                r = 2 * col + b
                r = 15 - r if rev else r
                to_relay(is_h, r, jnp.int32(c), mine_h.at[b], cand_v.at[4 + edge_h * 2 + rev], 0)

    def elsewhere(r, c):
        return jnp.logical_or(r != row, c != col)

    def face_at(step):
        return lax.rem(face + step, 6)

    barrier = pltpu.get_barrier_semaphore()

    def signal(dev):
        pl.semaphore_signal(barrier, inc=1, device_id=dev, device_id_type=MESH)

    def count(condition):
        return jnp.where(condition, 1, 0)

    arrivals = jnp.int32(0)
    for condition, dev, *_ in halo:
        pl.when(condition)(functools.partial(signal, dev))
        arrivals += count(condition)
    for role, r, c, *_ in relay:
        condition = jnp.logical_and(role, elsewhere(r, c))
        pl.when(condition)(functools.partial(signal, device(r, c)))
        arrivals += count(condition)
    for role in (is_v, is_h):
        @pl.when(role)
        def _():
            for step in range(1, 6):
                signal((group, face_at(step), tile))
        arrivals += 5 * count(role)

    def at(partner, y, x):
        f, z = jnp.where(partner == 1, pair_face, face), jnp.where(partner == 1, pair_half, half)
        return (group, f, lax.rem(tile_y + y, 8) * 8 + lax.rem(tile_x + x, 4) * 2 + z)

    for x in range(1, 4):
        signal(at(0, 0, x))
    for y in range(1, 8):
        signal(at(0, y, 0))
    signal(at(1, 0, 0))
    arrivals += 11

    wide[:, 256:] = jnp.zeros((CELLS, PAD - 256), F32)
    wide[:, :WIDE] = q_ref[...]
    q = wide[...]
    spread_winds[:, 2 * LEV :] = jnp.zeros((CELLS, PAD - 2 * LEV), F32)
    spread_winds[:, : 2 * LEV] = w_ref[...]
    winds = spread_winds[...]
    turned = [pltpu.roll(winds, (n * LEV) % PAD, 1) for n in (-1, 0, 1, 2, 3)]
    lane = iota((CELLS, PAD), 1)

    def repeat(first_turn):
        value = jnp.where(lane < WIDE, turned[first_turn + 3], 0.0)
        for n in (2, 1, 0):
            value = jnp.where(lane < (n + 1) * LEV, turned[first_turn + n], value)
        return value

    u, v = repeat(1), repeat(0)
    east, west = jnp.maximum(u, 0.0) * q, jnp.minimum(u, 0.0) * q
    north, south = jnp.maximum(v, 0.0) * q, jnp.minimum(v, 0.0) * q
    r8, c8 = iota((ROWS, CELLS), 0), iota((ROWS, CELLS), 1)
    strip_v[0] = dot(onehot(c8 == r8 * COLS), (-west).astype(BF16)).astype(BF16)
    strip_v[1] = dot(onehot(c8 == r8 * COLS + COLS - 1), east.astype(BF16)).astype(BF16)
    for b in (0, 1):
        strip_h[0, b] = (-south[8 * b : 8 * b + 8]).astype(BF16)
        strip_h[1, b] = north[CELLS - 16 + 8 * b : CELLS - 8 + 8 * b].astype(BF16)

    pl.semaphore_wait(barrier, arrivals)
    for x in range(1, 4):
        pl.semaphore_signal(lines.at[0], inc=1, device_id=at(0, 0, x), device_id_type=MESH)

    def copy(source, target, send, recv, dev):
        return pltpu.make_async_remote_copy(
            src_ref=source, dst_ref=target, send_sem=send, recv_sem=recv, device_id=dev, device_id_type=MESH
        )

    for role, r, c, source, target, send, recv in relay:
        @pl.when(jnp.logical_and(role, elsewhere(r, c)))
        def _():
            copy(source, target, send, recv, device(r, c)).start()

        @pl.when(jnp.logical_and(role, jnp.logical_not(elsewhere(r, c))))
        def _():
            pltpu.make_async_copy(source, target, recv).start()

    for condition, dev, source, target, send, recv in halo:
        @pl.when(condition)
        def _():
            copy(source, target, send, recv, dev).start()

    column = iota((CELLS, PAD), 0) % COLS
    zero16 = jnp.zeros((COLS, PAD), F32)
    east_in = jnp.where(column == 0, 0.0, pltpu.roll(east, 1, 0))
    west_in = jnp.where(column == COLS - 1, 0.0, pltpu.roll(west, CELLS - 1, 0))
    north_in = jnp.concatenate([zero16, north[: CELLS - COLS]], axis=0)
    south_in = jnp.concatenate([south[COLS:], zero16], axis=0)
    partial = q - ((east + west_in) - (east_in + west)) - ((north + south_in) - (north_in + south))

    owner_row = owner_ref[...].astype(F32)
    ii, jj = iota((CELLS, CELLS), 0), iota((CELLS, CELLS), 1)
    owner_col = jnp.sum(jnp.where(ii == jj, owner_row, 0.0), axis=1, keepdims=True)
    same = owner_col == owner_row
    rank_col = jnp.sum(jnp.where(jnp.logical_and(same, jj < ii), 1.0, 0.0), axis=1, keepdims=True)
    rank_row = jnp.sum(jnp.where(jnp.logical_and(same, ii < jj), 1.0, 0.0), axis=0, keepdims=True)
    slot_col = owner_col * CAP + rank_col
    slot_row = owner_row * CAP + rank_row
    gather = onehot(iota((SLOTS, CELLS), 0).astype(F32) == slot_row)
    spread = onehot(iota((CELLS, SLOTS), 1).astype(F32) == slot_col)

    def select(edge, length, total):
        pos = iota((length, total), 0)
        cand = iota((length, total), 1)
        parts = []
        for target in range(6):
            source_face, source_edge, rev = (links[n, edge, target] for n in range(3))
            start = (source_edge * 2 + rev) * length + rev * (length - 1)
            start = jnp.where(source_face == face, start, -1000)
            parts.append(onehot(cand == start + (1 - 2 * rev) * pos))
        return jnp.concatenate(parts, axis=0)

    def faces(fwd, rim, send, recv):
        for step in range(1, 6):
            other = face_at(step)
            copy(fwd.at[other], rim.at[face], send.at[step], recv, (group, other, tile)).start()
        pltpu.make_async_copy(fwd.at[face], rim.at[face], recv).start()

    @pl.when(is_v)
    def _():
        pltpu.make_async_copy(cand_v, cand_v, cand_recv.at[0]).wait()
        chosen = dot(select(edge_v, 8, 64), cand_v[...].reshape(64, PAD)).astype(BF16)
        fwd_v[...] = chosen.reshape(6, 8, PAD)
        faces(fwd_v, rim_v, rim_send_v, rim_recv.at[0])

    @pl.when(is_h)
    def _():
        pltpu.make_async_copy(cand_h, cand_h, cand_recv.at[1]).wait()
        chosen = dot(select(2 + edge_h, 16, 128), cand_h[...].reshape(128, PAD)).astype(BF16)
        fwd_h[...] = chosen.reshape(6, 2, 8, PAD)
        faces(fwd_h, rim_h, rim_send_h, rim_recv.at[1])

    pl.semaphore_wait(lines.at[0], 3)
    for y in range(1, 8):
        pl.semaphore_signal(lines.at[1], inc=1, device_id=at(0, y, 0), device_id_type=MESH)

    for (condition, *_), target, recv in zip(
        halo, (ghost_v.at[0], ghost_v.at[1], ghost_h.at[0], ghost_h.at[1]), (0, 1, 2, 3)
    ):
        @pl.when(condition)
        def _():
            pltpu.make_async_copy(target, target, halo_recv.at[recv]).wait()

    @pl.when(is_v)
    def _():
        pltpu.make_async_copy(rim_v, rim_v, rim_recv.at[0]).wait()
        ghost_v[edge_v] = jnp.sum(rim_v[...].astype(F32), axis=0).astype(BF16)

    @pl.when(is_h)
    def _():
        pltpu.make_async_copy(rim_h, rim_h, rim_recv.at[1]).wait()
        ghost_h[edge_h] = jnp.sum(rim_h[...].astype(F32), axis=0).astype(BF16)

    cell16, pos16 = iota((CELLS, 16), 0), iota((CELLS, 16), 1)
    side = jnp.where(pos16 < 8, pos16 * COLS, (pos16 - 8) * COLS + COLS - 1)
    advected = (
        partial
        + dot(onehot(cell16 == side), ghost_v[...].reshape(16, PAD))
        + dot(onehot(cell16 == pos16), ghost_h[0].reshape(16, PAD))
        + dot(onehot(cell16 == pos16 + CELLS - COLS), ghost_h[1].reshape(16, PAD))
    )
    gap = jnp.zeros((CELLS, FPAD - PAD), F32)
    change = pltpu.roll(jnp.concatenate([advected - q, gap], axis=1), WIDE, 1)
    features = jnp.where(iota((CELLS, FPAD), 1) < WIDE, jnp.concatenate([advected, gap], axis=1), change)
    outbox[...] = dot(gather, features.astype(BF16)).astype(BF16).reshape(TILES, CAP, FPAD)

    chip = tile_y * 4 + tile_x
    pl.semaphore_wait(lines.at[1], 7)

    def exchange(box, target, box_index, target_index, send, recv, meanwhile):
        def remote(y, x, partner):
            dev = at(partner, y, x)
            there = dev[2] // 2
            return copy(box.at[box_index(there, partner)], target.at[target_index(partner)], send, recv, dev)

        def step(i, carry):
            remote(1 + i // 8, (i // 2) % 4, 1 - i % 2).start()
            return carry

        lax.fori_loop(0, 57, step, 0)
        lax.fori_loop(58, TILES, step, 0)
        pltpu.make_async_copy(box.at[box_index(chip, 0)], target.at[target_index(0)], recv).start()
        meanwhile()
        pltpu.make_async_copy(target, target, recv).wait()

    def expert(there, partner):
        return there * 2 + jnp.where(partner == 1, 1 - half, half)

    def block(there, partner):
        return partner * 32 + there

    def sent(box, send):
        most = box.at[pl.ds(0, TILES - 1)]
        pltpu.make_async_copy(most, most, send).wait()

    def drain():
        for role, r, c, source, target, send, recv in relay:
            @pl.when(jnp.logical_and(role, elsewhere(r, c)))
            def _():
                copy(source, target, send, recv, device(r, c)).wait_send()
        for condition, dev, source, target, send, recv in halo:
            @pl.when(condition)
            def _():
                copy(source, target, send, recv, dev).wait_send()
        for role, fwd, rim, send in ((is_v, fwd_v, rim_v, rim_send_v), (is_h, fwd_h, rim_h, rim_send_h)):
            @pl.when(role)
            def _():
                for step in range(1, 6):
                    other = face_at(step)
                    copy(fwd.at[other], rim.at[face], send.at[step], rim_recv.at[0], (group, other, tile)).wait_send()
        for source, target, n in weights:
            pltpu.make_async_copy(source, target, wsem.at[n]).wait()

    exchange(outbox, inbox, expert, lambda partner: block(chip, partner), a2a_send, a2a_recv, drain)
    x = inbox[...].reshape(SLOTS, FPAD)[:, :FEAT]
    hidden = silu(dot(x, first[...])).astype(BF16)
    hidden = silu(dot(hidden, middle[...])).astype(BF16)
    out = lax.dot_general(hidden, last[...], (((1,), (1,)), ((), ())), preferred_element_type=F32)
    reply[:, :, :WIDE] = out.astype(BF16).reshape(TILES, CAP, WIDE)
    exchange(
        reply, answers, block, lambda partner: expert(chip, 0), ret_send, ret_recv, lambda: sent(outbox, a2a_send)
    )
    tendency = dot(spread, answers[...].reshape(SLOTS, PAD))
    out_ref[...] = (advected + tendency)[:, :WIDE]

    sent(reply, ret_send)


def local(tracers, wind_field, face_links, owner_map, first_layer, middle_layer, last_layer):
    vmem = pl.BlockSpec(memory_space=pltpu.VMEM)
    smem = pl.BlockSpec(memory_space=pltpu.SMEM)
    hbm = pl.BlockSpec(memory_space=pl.ANY)
    dma = pltpu.SemaphoreType.DMA
    updated = pl.pallas_call(
        kernel,
        out_shape=jax.ShapeDtypeStruct((CELLS, WIDE), F32),
        in_specs=[vmem, vmem, smem, vmem, hbm, hbm, hbm],
        out_specs=vmem,
        scratch_shapes=[
            pltpu.VMEM(first_layer.shape[1:], BF16),
            pltpu.VMEM(middle_layer.shape[1:], BF16),
            pltpu.VMEM(last_layer.shape[:0:-1], BF16),
            pltpu.VMEM((2, 8, PAD), BF16),
            pltpu.VMEM((2, 2, 8, PAD), BF16),
            pltpu.VMEM((2, 8, PAD), BF16),
            pltpu.VMEM((2, 2, 8, PAD), BF16),
            pltpu.VMEM((8, 8, PAD), BF16),
            pltpu.VMEM((8, 2, 8, PAD), BF16),
            pltpu.VMEM((6, 8, PAD), BF16),
            pltpu.VMEM((6, 2, 8, PAD), BF16),
            pltpu.VMEM((6, 8, PAD), BF16),
            pltpu.VMEM((6, 2, 8, PAD), BF16),
            pltpu.VMEM((CELLS, PAD), F32),
            pltpu.VMEM((CELLS, PAD), F32),
            pltpu.VMEM((TILES, CAP, FPAD), BF16),
            pltpu.VMEM((TILES, CAP, FPAD), BF16),
            pltpu.VMEM((TILES, CAP, PAD), BF16),
            pltpu.VMEM((TILES, CAP, PAD), BF16),
            dma((3,)),
            dma((4,)),
            dma((4,)),
            dma((20,)),
            dma((2,)),
            dma((6,)),
            dma((6,)),
            dma((2,)),
            dma, dma, dma, dma,
            pltpu.SemaphoreType.REGULAR((2,)),
        ],
        compiler_params=pltpu.CompilerParams(collective_id=0, has_side_effects=True),
    )(
        tracers.reshape(CELLS, WIDE),
        wind_field.reshape(CELLS, 2 * LEV),
        face_links.transpose(2, 1, 0),
        owner_map.reshape(1, CELLS),
        first_layer[0],
        middle_layer[0],
        last_layer[0].T,
    )
    return updated.reshape(tracers.shape)


def solution(mesh):
    in_specs = (
        P("face", ("group", "tile"), None, None, None),
        P("face", ("group", "tile"), None, None, None),
        P(),
        P("face", ("group", "tile"), None, None),
        P("tile", None, None),
        P("tile", None, None),
        P("tile", None, None),
    )
    out_specs = P("face", ("group", "tile"), None, None, None)
    return jax.shard_map(local, mesh=mesh, in_specs=in_specs, out_specs=out_specs, check_vma=False)
```
